32 devices in a mesh: code: 4 (over y, core), vocab: 8 (over z, x).
Axes of the slice: x: 2, y: 2, z: 4, core: 2. Of those that a mesh axis runs over, the one named last changes fastest.
Arguments:
- latent_activations: bfloat16 [512, 8192], P(None, 'vocab'), may hold values from -150 to 150
- code_fragments: bfloat16 [4, 5344, 8192], P('code', 'vocab'), may hold values from -0.25 to 0.25
- remaining_fragments: int32 [8, 2], P('vocab'), may hold values from 0 to 3, as said below
Outputs:
- log_probs: float32 [512, 10688], P('code', 'vocab')
The draws below stay inside these ranges and needn't reach their ends.
Inputs may be any that keep to these rules, and one draw needn't show every extreme that they name: `remaining_fragments`: each row holds 2 different share numbers in increasing order.
All inputs are finite; a program needn't handle non-finite values.
Results may differ from the reference program's by a relative error of at most 0.0003.
Values may be sent and summed in bfloat16 or wider, within the bound.
A program may use at most 128 MiB of HBM per device.

```python
import jax
import jax.numpy as jnp
from jax import lax

D = 8192
ROWS = 668
BATCH = 512
SHARES = 4
DATA = 2
GROUPS = 8
VOCAB = 10688


def draw_latent_activations(key, part):
    first_key, second_key = jax.random.split(jax.random.fold_in(key, 11))
    standard = jax.random.truncated_normal(first_key, -5.0, 5.0, (BATCH, D), jnp.float32)
    row_scale = jnp.exp(jax.random.uniform(second_key, (BATCH, 1), jnp.float32, jnp.log(0.75), jnp.log(6.0)))
    return (standard * row_scale).astype(jnp.bfloat16)


def draw_remaining_fragments(key, part):
    scores = jax.random.randint(jax.random.fold_in(key, 5), (GROUPS, SHARES), 0, 1 << 20) * SHARES
    scores = scores + jnp.arange(SHARES, dtype=jnp.int32)[None, :]
    ordering = jnp.argsort(scores, axis=1, stable=True)
    return jnp.sort(ordering[:, :DATA], axis=1).astype(jnp.int32)


def shard_levels(stream_key, extent, shards, least, high):
    level, own = 1.0, jax.random.fold_in(stream_key, 6)
    for position, blocks in shards:
        draws = jnp.exp(jax.random.uniform(jax.random.fold_in(own, position), (blocks,), jnp.float32, least / len(shards), high / len(shards)))
        level = level * jnp.repeat(draws, extent[position] // blocks).reshape([-1 if axis == position else 1 for axis in range(len(extent))])
    return level


def noise(key, shape, spread, bound, pieces=(), held_as=jnp.bfloat16):
    drawn = jax.random.normal(key, shape, jnp.float32) * spread
    if len(pieces) > 0:
        drawn = shard_levels(key, shape, pieces, -0.22, 0.18) * drawn
    return jnp.clip(drawn, min=-bound, max=bound).astype(held_as)


def setup_inputs(seed: int = 0) -> dict:
    arg_keys = jax.random.split(jax.random.key(seed), 4)
    return {
        "latent_activations": draw_latent_activations(jax.random.fold_in(arg_keys[3], 71), 0),
        "code_fragments": noise(arg_keys[1], (SHARES, GROUPS * ROWS, D), (D // 16) ** -0.5, 0.25, ((0, 4), (1, 8))),
        "remaining_fragments": draw_remaining_fragments(jax.random.fold_in(arg_keys[3], 71), 0),
    }


def generator(count):
    nodes = jnp.cos(jnp.pi * (jnp.arange(count).astype(jnp.float32) + 0.5) / count)
    return jnp.concatenate([jnp.eye(count, dtype=jnp.float32), jnp.ones((1, count), jnp.float32), nodes[None, :]], axis=0)

def restoring_operator(chosen_row):
    select = (chosen_row[:, None] == jnp.arange(SHARES).astype(jnp.int32)[None, :]).astype(jnp.float32)
    square = jnp.dot(select, generator(DATA), precision=lax.Precision.HIGHEST)
    inverse = jnp.linalg.inv(square)
    return jnp.dot(inverse, select, precision=lax.Precision.HIGHEST)

def reference(latent_activations, code_fragments, remaining_fragments):
    blocks = code_fragments.reshape(SHARES, GROUPS, ROWS, D)

    def group_logits(fragment_position):
        block = blocks[:, fragment_position].reshape(SHARES * ROWS, D)
        encoded = jnp.dot(latent_activations.astype(jnp.float32), block.T.astype(jnp.float32), preferred_element_type=jnp.float32)
        encoded = encoded.reshape(BATCH, SHARES, ROWS)
        restored_lines = restoring_operator(remaining_fragments[fragment_position])
        payload_rows = jnp.einsum('js,bsr->bjr', restored_lines, encoded, precision=lax.Precision.HIGHEST)
        return payload_rows.reshape(BATCH, DATA * ROWS)
    logits = lax.map(group_logits, jnp.arange(GROUPS).astype(jnp.int32))
    logits = jnp.transpose(logits, (1, 0, 2)).reshape(BATCH, VOCAB)
    top = jnp.max(logits, axis=1, keepdims=True)
    total = jnp.sum(jnp.exp(logits - top), axis=1, keepdims=True)
    return logits - (top + jnp.log(total))
```

```python
import functools
import math

import jax
import jax.numpy as jnp
from jax import lax
from jax.experimental import pallas as pl
from jax.experimental.pallas import tpu as pltpu
from jax.sharding import PartitionSpec as P

MESH = pl.DeviceIdType.MESH


def ring_order(count):
    outer = 4 if count % 4 == 0 else 1
    inner = count // outer
    if outer == 1 or inner == 1:
        return list(range(count))
    walk = [(0, 0)]
    for row in range(outer):
        columns = range(1, inner) if row % 2 == 0 else range(inner - 1, 0, -1)
        walk += [(row, column) for column in columns]
    walk += [(row, 0) for row in range(outer - 1, 0, -1)]
    return [row * inner + column for row, column in walk]


def decode_table(alive, data):
    nodes = [math.cos(math.pi * (j + 0.5) / data) for j in range(data)]
    lost = [1.0 - alive[j] for j in range(data)]
    lost_count = sum(lost)
    single = jnp.where(lost_count < 1.5, 1.0, 0.0)
    by_ones = single * alive[data]
    by_nodes = single * alive[data + 1]
    double = 1.0 - single
    table = []
    for j in range(data):
        row = [None] * (data + 2)
        gaps = [(b, double * lost[b]) for b in range(data) if b != j]
        for s in range(data):
            if s == j:
                row[s] = alive[j]
                continue
            value = -by_ones - by_nodes * (nodes[s] / nodes[j])
            for b, on in gaps:
                if b != s:
                    value = value + on * ((nodes[b] - nodes[s]) / (nodes[j] - nodes[b]))
            row[s] = lost[j] * alive[s] * value
        ones_value, nodes_value = by_ones, by_nodes * (1.0 / nodes[j])
        for b, on in gaps:
            ones_value = ones_value - on * (nodes[b] / (nodes[j] - nodes[b]))
            nodes_value = nodes_value + on * (1.0 / (nodes[j] - nodes[b]))
        row[data] = lost[j] * ones_value
        row[data + 1] = lost[j] * nodes_value
        table.append(row)
    return table


def kernel(
    codes, vocabs, order, subs,
    left_ref, x_ref, w_ref, out_ref,
    lat, wbuf, enc, rx, stat_tx, stat_rx,
    w_sem, x_sem, ring_send, ring_recv, pair_send, pair_recv, tx_sem, rx_sem, st_send, st_recv,
):
    me = lax.axis_index("code")
    v = lax.axis_index("vocab")
    batch, depth = x_ref.shape
    share_rows = w_ref.shape[1]
    rows = batch // codes
    phases = codes // 2
    data = left_ref.shape[1]
    half = vocabs // 2
    core = lax.rem(me, 2)
    sgn = 1 - 2 * core
    partner = me + sgn

    pos = jnp.int32(0)
    for i in range(vocabs):
        pos = pos + jnp.where(v == order[i], i, 0)

    def place(shift):
        return lax.rem(pos + shift + 2 * vocabs, vocabs)

    def device_at(where):
        found = jnp.int32(0)
        for i in range(vocabs):
            found = found + jnp.where(where == i, order[i], 0)
        return found

    ahead = device_at(place(sgn))
    behind = device_at(place(-sgn))

    for i in range(vocabs):
        pltpu.make_async_copy(
            w_ref.at[0, :, pl.ds(order[i] * depth, depth)], wbuf.at[i], w_sem.at[i]
        ).start()
    own_copy = pltpu.make_async_copy(x_ref, lat.at[pos], x_sem.at[0])
    own_copy.start()

    barrier = pltpu.get_barrier_semaphore()
    for k in range(1, codes):
        pl.semaphore_signal(barrier, inc=1, device_id={"code": lax.rem(me + k, codes)}, device_id_type=MESH)
    for k in range(1, vocabs):
        pl.semaphore_signal(barrier, inc=1, device_id={"vocab": lax.rem(v + k, vocabs)}, device_id_type=MESH)
    pl.semaphore_wait(barrier, codes + vocabs - 2)

    piece = rows // 2
    many = 2 // subs

    def piece_rows(phase, sub, which):
        start = (sub * phases + phase) * rows + which * piece
        return pl.ds(pl.multiple_of(start, 16), piece)

    def slot(phase, sub, way, d):
        return ((phase * 2 + sub) * 2 + way) * half + d - 1

    def ring_copy(phase, sub, way, d):
        source_place = place(-sgn * (d - 1)) if way == 0 else place(sgn * (d - 1))
        rs = piece_rows(phase, sub, core)
        src = x_ref.at[rs, :] if d == 1 else lat.at[source_place, rs, :]
        return pltpu.make_async_remote_copy(
            src_ref=src,
            dst_ref=lat.at[source_place, rs, :],
            send_sem=ring_send.at[slot(phase, sub, way, d)],
            recv_sem=ring_recv.at[slot(phase, sub, way, d)],
            device_id={"vocab": ahead if way == 0 else behind},
            device_id_type=MESH,
        )

    def arrival(phase, sub, way, d):
        source_place = place(-sgn * d) if way == 0 else place(sgn * d)
        rs = piece_rows(phase, sub, core)
        return pltpu.make_async_remote_copy(
            src_ref=lat.at[source_place, rs, :],
            dst_ref=lat.at[source_place, rs, :],
            send_sem=ring_send.at[slot(phase, sub, way, d)],
            recv_sem=ring_recv.at[slot(phase, sub, way, d)],
            device_id={"vocab": ahead if way == 0 else behind},
            device_id_type=MESH,
        )

    def pair_copy(phase, sub, way, d):
        source_place = place(-sgn * d) if way == 0 else place(sgn * d)
        rs = piece_rows(phase, sub, core)
        return pltpu.make_async_remote_copy(
            src_ref=lat.at[source_place, rs, :],
            dst_ref=lat.at[source_place, rs, :],
            send_sem=pair_send.at[slot(phase, sub, way, d)],
            recv_sem=pair_recv.at[slot(phase, sub, way, d)],
            device_id={"code": partner},
            device_id_type=MESH,
        )

    def pair_arrival(phase, sub, way, d):
        source_place = place(sgn * d) if way == 0 else place(-sgn * d)
        rs = piece_rows(phase, sub, 1 - core)
        return pltpu.make_async_remote_copy(
            src_ref=lat.at[source_place, rs, :],
            dst_ref=lat.at[source_place, rs, :],
            send_sem=pair_send.at[slot(phase, sub, way, d)],
            recv_sem=pair_recv.at[slot(phase, sub, way, d)],
            device_id={"code": partner},
            device_id_type=MESH,
        )

    def reach(way):
        return half if way == 0 else half - 1

    sends = []

    def begin(phase):
        for sub in range(2):
            for way in range(2):
                if reach(way) >= 1:
                    copy = ring_copy(phase, sub, way, 1)
                    copy.start()
                    sends.append(copy)

    def multiply(phase, where, first):
        for sub in range(2):
            block = sub * phases + phase
            part = lax.dot_general(
                lat[where, pl.ds(block * rows, rows), :],
                wbuf[where],
                (((1,), (1,)), ((), ())),
                preferred_element_type=jnp.float32,
            )
            enc[block] = part if first else enc[block] + part

    def take(phase, d):
        for sub in range(2):
            for way in range(2):
                if d <= reach(way):
                    pair_arrival(phase, sub, way, d).wait_recv()
        multiply(phase, place(-sgn * d), False)
        if d < half:
            multiply(phase, place(sgn * d), False)

    begin(0)
    own_copy.wait()
    for i in range(vocabs):
        pltpu.make_async_copy(
            w_ref.at[0, :, pl.ds(order[i] * depth, depth)], wbuf.at[i], w_sem.at[i]
        ).wait()

    for phase in range(phases):
        multiply(phase, pos, True)
        for d in range(1, half + 1):
            for sub in range(2):
                for way in range(2):
                    if d > reach(way):
                        continue
                    arrival(phase, sub, way, d).wait_recv()
                    if d < reach(way):
                        onward = ring_copy(phase, sub, way, d + 1)
                        onward.start()
                        sends.append(onward)
                    across = pair_copy(phase, sub, way, d)
                    across.start()
                    sends.append(across)
            if d == max(half - 1, 1) and phase + 1 < phases:
                begin(phase + 1)
            if d > 1:
                take(phase, d - 1)
        take(phase, half)
        for sub in range(2):
            block = sub * phases + phase

            @pl.when(me != block)
            def _():
                pltpu.make_async_remote_copy(
                    src_ref=enc.at[block],
                    dst_ref=rx.at[me],
                    send_sem=tx_sem.at[block],
                    recv_sem=rx_sem.at[me],
                    device_id={"code": jnp.int32(block)},
                    device_id_type=MESH,
                ).start()

    rx[me] = enc[me]

    alive = []
    for s in range(codes):
        here = jnp.int32(0)
        for k in range(data):
            here = here + jnp.where(left_ref[0, k] == s, 1, 0)
        alive.append(here.astype(jnp.float32))
    table = decode_table(alive, data)

    for k in range(1, codes):
        other = lax.rem(me + k, codes)
        pltpu.make_async_remote_copy(
            src_ref=enc.at[0],
            dst_ref=rx.at[other],
            send_sem=tx_sem.at[other],
            recv_sem=rx_sem.at[other],
            device_id={"code": other},
            device_id_type=MESH,
        ).wait_recv()

    top = None
    logits = []
    for j in range(data):
        value = table[j][0] * rx[0]
        for s in range(1, codes):
            value = value + table[j][s] * rx[s]
        logits.append(value)
        out_ref[:, j * share_rows:(j + 1) * share_rows] = value
        peak = jnp.max(value, axis=1, keepdims=True)
        top = peak if top is None else jnp.maximum(top, peak)
    total = None
    for j in range(data):
        part = jnp.sum(jnp.exp(logits[j] - top), axis=1, keepdims=True)
        total = part if total is None else total + part

    lane = lax.broadcasted_iota(jnp.int32, (rows, 128), 1)
    both = jnp.where(lane == 0, top, total)
    stat_tx[...] = jnp.transpose(both)[:8, :]
    stat_rx[v] = stat_tx[...]
    stat_sends = []
    for k in range(1, vocabs):
        copy = pltpu.make_async_remote_copy(
            src_ref=stat_tx,
            dst_ref=stat_rx.at[v],
            send_sem=st_send.at[k],
            recv_sem=st_recv.at[v],
            device_id={"vocab": lax.rem(v + k, vocabs)},
            device_id_type=MESH,
        )
        copy.start()
        stat_sends.append(copy)
    for copy in sends:
        copy.wait_send()
    for k in range(1, codes):
        other = lax.rem(me + k, codes)
        pltpu.make_async_remote_copy(
            src_ref=enc.at[0],
            dst_ref=rx.at[other],
            send_sem=tx_sem.at[other],
            recv_sem=rx_sem.at[other],
            device_id={"code": other},
            device_id_type=MESH,
        ).wait_send()
    for k in range(1, vocabs):
        other = lax.rem(v + k, vocabs)
        pltpu.make_async_remote_copy(
            src_ref=stat_tx,
            dst_ref=stat_rx.at[other],
            send_sem=st_send.at[k],
            recv_sem=st_recv.at[other],
            device_id={"vocab": other},
            device_id_type=MESH,
        ).wait_recv()

    stats = stat_rx[...]
    tops, totals = stats[:, 0:1, :], stats[:, 1:2, :]
    peak = jnp.max(tops, axis=0)
    whole = jnp.sum(totals * jnp.exp(tops - peak[None]), axis=0)
    normalizer = jnp.transpose(jnp.broadcast_to(peak + jnp.log(whole), (128, rows)))[:, 0:1]
    out_ref[...] = out_ref[...] - normalizer
    for copy in stat_sends:
        copy.wait_send()


def solution(mesh):
    codes, vocabs = mesh.shape["code"], mesh.shape["vocab"]
    order = ring_order(vocabs)

    def shards(latent_activations, code_fragments, remaining_fragments):
        batch, depth = latent_activations.shape
        share_rows = code_fragments.shape[1]
        data = remaining_fragments.shape[1]
        rows = batch // codes
        slots = (codes // 2) * 2 * 2 * (vocabs // 2)
        dma = pltpu.SemaphoreType.DMA
        return pl.pallas_call(
            functools.partial(kernel, codes, vocabs, order, 1),
            out_shape=jax.ShapeDtypeStruct((rows, data * share_rows), jnp.float32),
            in_specs=[
                pl.BlockSpec(memory_space=pltpu.SMEM),
                pl.BlockSpec(memory_space=pl.ANY),
                pl.BlockSpec(memory_space=pl.ANY),
            ],
            out_specs=pl.BlockSpec(memory_space=pltpu.VMEM),
            scratch_shapes=[
                pltpu.VMEM((vocabs, batch, depth), jnp.bfloat16),
                pltpu.VMEM((vocabs, share_rows, depth), jnp.bfloat16),
                pltpu.VMEM((codes, rows, share_rows), jnp.float32),
                pltpu.VMEM((codes, rows, share_rows), jnp.float32),
                pltpu.VMEM((8, rows), jnp.float32),
                pltpu.VMEM((vocabs, 8, rows), jnp.float32),
                dma((vocabs,)),
                dma((1,)),
                dma((slots,)),
                dma((slots,)),
                dma((slots,)),
                dma((slots,)),
                dma((codes,)),
                dma((codes,)),
                dma((vocabs,)),
                dma((vocabs,)),
            ],
            compiler_params=pltpu.CompilerParams(collective_id=0, has_side_effects=True),
        )(remaining_fragments, latent_activations, code_fragments)

    return jax.shard_map(
        shards,
        mesh=mesh,
        in_specs=(P(None, "vocab"), P("code", "vocab", None), P("vocab", None)),
        out_specs=P("code", "vocab"),
        check_vma=False,
    )
```

```python
import functools
import math

import jax
import jax.numpy as jnp
from jax import lax
from jax.experimental import pallas as pl
from jax.experimental.pallas import tpu as pltpu
from jax.sharding import PartitionSpec as P

MESH = pl.DeviceIdType.MESH


def ring_order(count):
    outer = 4 if count % 4 == 0 else 1
    inner = count // outer
    if outer == 1 or inner == 1:
        return list(range(count))
    walk = [(0, 0)]
    for row in range(outer):
        columns = range(1, inner) if row % 2 == 0 else range(inner - 1, 0, -1)
        walk += [(row, column) for column in columns]
    walk += [(row, 0) for row in range(outer - 1, 0, -1)]
    return [row * inner + column for row, column in walk]


def decode_table(alive, data):
    nodes = [math.cos(math.pi * (j + 0.5) / data) for j in range(data)]
    lost = [1.0 - alive[j] for j in range(data)]
    lost_count = sum(lost)
    single = jnp.where(lost_count < 1.5, 1.0, 0.0)
    by_ones = single * alive[data]
    by_nodes = single * alive[data + 1]
    double = 1.0 - single
    table = []
    for j in range(data):
        row = [None] * (data + 2)
        gaps = [(b, double * lost[b]) for b in range(data) if b != j]
        for s in range(data):
            if s == j:
                row[s] = alive[j]
                continue
            value = -by_ones - by_nodes * (nodes[s] / nodes[j])
            for b, on in gaps:
                if b != s:
                    value = value + on * ((nodes[b] - nodes[s]) / (nodes[j] - nodes[b]))
            row[s] = lost[j] * alive[s] * value
        ones_value, nodes_value = by_ones, by_nodes * (1.0 / nodes[j])
        for b, on in gaps:
            ones_value = ones_value - on * (nodes[b] / (nodes[j] - nodes[b]))
            nodes_value = nodes_value + on * (1.0 / (nodes[j] - nodes[b]))
        row[data] = lost[j] * ones_value
        row[data + 1] = lost[j] * nodes_value
        table.append(row)
    return table


def kernel(
    codes, vocabs, order, subs,
    left_ref, x_ref, w_ref, out_ref,
    lat, wbuf, enc, rx, stat_tx, stat_rx,
    w_sem, x_sem, ring_send, ring_recv, pair_send, pair_recv, tx_sem, rx_sem, st_send, st_recv,
):
    me = lax.axis_index("code")
    v = lax.axis_index("vocab")
    batch, depth = x_ref.shape
    share_rows = w_ref.shape[1]
    rows = batch // codes
    phases = codes // 2
    data = left_ref.shape[1]
    half = vocabs // 2
    core = lax.rem(me, 2)
    sgn = 1 - 2 * core
    partner = me + sgn

    pos = jnp.int32(0)
    for i in range(vocabs):
        pos = pos + jnp.where(v == order[i], i, 0)

    def place(shift):
        return lax.rem(pos + shift + 2 * vocabs, vocabs)

    def device_at(where):
        found = jnp.int32(0)
        for i in range(vocabs):
            found = found + jnp.where(where == i, order[i], 0)
        return found

    ahead = device_at(place(sgn))
    behind = device_at(place(-sgn))

    for i in range(vocabs):
        pltpu.make_async_copy(
            w_ref.at[0, :, pl.ds(order[i] * depth, depth)], wbuf.at[i], w_sem.at[i]
        ).start()
    own_copy = pltpu.make_async_copy(x_ref, lat.at[pos], x_sem.at[0])
    own_copy.start()

    barrier = pltpu.get_barrier_semaphore()
    for k in range(1, codes):
        pl.semaphore_signal(barrier, inc=1, device_id={"code": lax.rem(me + k, codes)}, device_id_type=MESH)
    for neighbour in (ahead, behind):
        pl.semaphore_signal(barrier, inc=1, device_id={"vocab": neighbour}, device_id_type=MESH)
    pl.semaphore_wait(barrier, codes + 1)

    piece = rows // 2
    many = 2 // subs

    def piece_rows(phase, sub, which):
        start = (sub * phases + phase) * rows + which * piece
        return pl.ds(pl.multiple_of(start, 16), piece)

    def slot(phase, sub, way, d):
        return ((phase * 2 + sub) * 2 + way) * half + d - 1

    def ring_copy(phase, sub, way, d):
        source_place = place(-sgn * (d - 1)) if way == 0 else place(sgn * (d - 1))
        rs = piece_rows(phase, sub, core)
        src = x_ref.at[rs, :] if d == 1 else lat.at[source_place, rs, :]
        return pltpu.make_async_remote_copy(
            src_ref=src,
            dst_ref=lat.at[source_place, rs, :],
            send_sem=ring_send.at[slot(phase, sub, way, d)],
            recv_sem=ring_recv.at[slot(phase, sub, way, d)],
            device_id={"vocab": ahead if way == 0 else behind},
            device_id_type=MESH,
        )

    def arrival(phase, sub, way, d):
        source_place = place(-sgn * d) if way == 0 else place(sgn * d)
        rs = piece_rows(phase, sub, core)
        return pltpu.make_async_remote_copy(
            src_ref=lat.at[source_place, rs, :],
            dst_ref=lat.at[source_place, rs, :],
            send_sem=ring_send.at[slot(phase, sub, way, d)],
            recv_sem=ring_recv.at[slot(phase, sub, way, d)],
            device_id={"vocab": ahead if way == 0 else behind},
            device_id_type=MESH,
        )

    def pair_copy(phase, sub, way, d):
        source_place = place(-sgn * d) if way == 0 else place(sgn * d)
        rs = piece_rows(phase, sub, core)
        return pltpu.make_async_remote_copy(
            src_ref=lat.at[source_place, rs, :],
            dst_ref=lat.at[source_place, rs, :],
            send_sem=pair_send.at[slot(phase, sub, way, d)],
            recv_sem=pair_recv.at[slot(phase, sub, way, d)],
            device_id={"code": partner},
            device_id_type=MESH,
        )

    def pair_arrival(phase, sub, way, d):
        source_place = place(sgn * d) if way == 0 else place(-sgn * d)
        rs = piece_rows(phase, sub, 1 - core)
        return pltpu.make_async_remote_copy(
            src_ref=lat.at[source_place, rs, :],
            dst_ref=lat.at[source_place, rs, :],
            send_sem=pair_send.at[slot(phase, sub, way, d)],
            recv_sem=pair_recv.at[slot(phase, sub, way, d)],
            device_id={"code": partner},
            device_id_type=MESH,
        )

    def reach(way):
        return half if way == 0 else half - 1

    sends = []

    def begin(phase):
        for sub in range(2):
            for way in range(2):
                if reach(way) >= 1:
                    copy = ring_copy(phase, sub, way, 1)
                    copy.start()
                    sends.append(copy)

    def multiply(phase, where, first):
        hidden = [lat[where, pl.ds((sub * phases + phase) * rows, rows), :] for sub in range(2)]
        part = lax.dot_general(
            wbuf[where],
            jnp.concatenate(hidden, axis=0),
            (((1,), (1,)), ((), ())),
            preferred_element_type=jnp.float32,
        )
        for sub in range(2):
            block = sub * phases + phase
            mine = part[:, sub * rows:(sub + 1) * rows]
            enc[block] = mine if first else enc[block] + mine

    def take(phase, d):
        for sub in range(2):
            for way in range(2):
                if d <= reach(way):
                    pair_arrival(phase, sub, way, d).wait_recv()
        multiply(phase, place(-sgn * d), False)
        if d < half:
            multiply(phase, place(sgn * d), False)

    begin(0)
    own_copy.wait()
    for i in range(vocabs):
        pltpu.make_async_copy(
            w_ref.at[0, :, pl.ds(order[i] * depth, depth)], wbuf.at[i], w_sem.at[i]
        ).wait()

    for phase in range(phases):
        multiply(phase, pos, True)
        for d in range(1, half + 1):
            for sub in range(2):
                for way in range(2):
                    if d > reach(way):
                        continue
                    arrival(phase, sub, way, d).wait_recv()
                    if d < reach(way):
                        onward = ring_copy(phase, sub, way, d + 1)
                        onward.start()
                        sends.append(onward)
                    across = pair_copy(phase, sub, way, d)
                    across.start()
                    sends.append(across)
            if d == max(half - 1, 1) and phase + 1 < phases:
                begin(phase + 1)
            if d > 1:
                take(phase, d - 1)
        take(phase, half)
        for sub in range(2):
            block = sub * phases + phase

            @pl.when(me != block)
            def _():
                pltpu.make_async_remote_copy(
                    src_ref=enc.at[block],
                    dst_ref=rx.at[me],
                    send_sem=tx_sem.at[block],
                    recv_sem=rx_sem.at[me],
                    device_id={"code": jnp.int32(block)},
                    device_id_type=MESH,
                ).start()

    rx[me] = enc[me]

    alive = []
    for s in range(codes):
        here = jnp.int32(0)
        for k in range(data):
            here = here + jnp.where(left_ref[0, k] == s, 1, 0)
        alive.append(here.astype(jnp.float32))
    table = decode_table(alive, data)

    for k in range(1, codes):
        other = lax.rem(me + k, codes)
        pltpu.make_async_remote_copy(
            src_ref=enc.at[0],
            dst_ref=rx.at[other],
            send_sem=tx_sem.at[other],
            recv_sem=rx_sem.at[other],
            device_id={"code": other},
            device_id_type=MESH,
        ).wait_recv()

    top = None
    logits = []
    for j in range(data):
        value = table[j][0] * rx[0]
        for s in range(1, codes):
            value = value + table[j][s] * rx[s]
        logits.append(value)
        out_ref[j * share_rows:(j + 1) * share_rows, :] = value
        peak = jnp.max(value, axis=0, keepdims=True)
        top = peak if top is None else jnp.maximum(top, peak)
    total = None
    for j in range(data):
        part = jnp.sum(jnp.exp(logits[j] - top), axis=0, keepdims=True)
        total = part if total is None else total + part

    line = lax.broadcasted_iota(jnp.int32, (8, rows), 0)
    stat_tx[...] = jnp.where(line == 0, top, total)
    stat_rx[v] = stat_tx[...]
    stat_sends = []
    for k in range(1, vocabs):
        copy = pltpu.make_async_remote_copy(
            src_ref=stat_tx,
            dst_ref=stat_rx.at[v],
            send_sem=st_send.at[k],
            recv_sem=st_recv.at[v],
            device_id={"vocab": lax.rem(v + k, vocabs)},
            device_id_type=MESH,
        )
        copy.start()
        stat_sends.append(copy)
    for copy in sends:
        copy.wait_send()
    for k in range(1, codes):
        other = lax.rem(me + k, codes)
        pltpu.make_async_remote_copy(
            src_ref=enc.at[0],
            dst_ref=rx.at[other],
            send_sem=tx_sem.at[other],
            recv_sem=rx_sem.at[other],
            device_id={"code": other},
            device_id_type=MESH,
        ).wait_send()
    for k in range(1, vocabs):
        other = lax.rem(v + k, vocabs)
        pltpu.make_async_remote_copy(
            src_ref=stat_tx,
            dst_ref=stat_rx.at[other],
            send_sem=st_send.at[k],
            recv_sem=st_recv.at[other],
            device_id={"vocab": other},
            device_id_type=MESH,
        ).wait_recv()

    stats = stat_rx[...]
    tops, totals = stats[:, 0:1, :], stats[:, 1:2, :]
    peak = jnp.max(tops, axis=0)
    whole = jnp.sum(totals * jnp.exp(tops - peak[None]), axis=0)
    out_ref[...] = out_ref[...] - (peak + jnp.log(whole))
    for copy in stat_sends:
        copy.wait_send()


def solution(mesh):
    codes, vocabs = mesh.shape["code"], mesh.shape["vocab"]
    order = ring_order(vocabs)

    def shards(latent_activations, code_fragments, remaining_fragments):
        batch, depth = latent_activations.shape
        share_rows = code_fragments.shape[1]
        data = remaining_fragments.shape[1]
        rows = batch // codes
        slots = (codes // 2) * 2 * 2 * (vocabs // 2)
        dma = pltpu.SemaphoreType.DMA
        return pl.pallas_call(
            functools.partial(kernel, codes, vocabs, order, 1),
            out_shape=jax.ShapeDtypeStruct((data * share_rows, rows), jnp.float32),
            in_specs=[
                pl.BlockSpec(memory_space=pltpu.SMEM),
                pl.BlockSpec(memory_space=pl.ANY),
                pl.BlockSpec(memory_space=pl.ANY),
            ],
            out_specs=pl.BlockSpec(memory_space=pltpu.VMEM),
            scratch_shapes=[
                pltpu.VMEM((vocabs, batch, depth), jnp.bfloat16),
                pltpu.VMEM((vocabs, share_rows, depth), jnp.bfloat16),
                pltpu.VMEM((codes, share_rows, rows), jnp.float32),
                pltpu.VMEM((codes, share_rows, rows), jnp.float32),
                pltpu.VMEM((8, rows), jnp.float32),
                pltpu.VMEM((vocabs, 8, rows), jnp.float32),
                dma((vocabs,)),
                dma((1,)),
                dma((slots,)),
                dma((slots,)),
                dma((slots,)),
                dma((slots,)),
                dma((codes,)),
                dma((codes,)),
                dma((vocabs,)),
                dma((vocabs,)),
            ],
            compiler_params=pltpu.CompilerParams(collective_id=0, has_side_effects=True),
        )(remaining_fragments, latent_activations, code_fragments).T

    return jax.shard_map(
        shards,
        mesh=mesh,
        in_specs=(P(None, "vocab"), P("code", "vocab", None), P("vocab", None)),
        out_specs=P("code", "vocab"),
        check_vma=False,
    )
```

```python
import functools
import math

import jax
import jax.numpy as jnp
from jax import lax
from jax.experimental import pallas as pl
from jax.experimental.pallas import tpu as pltpu
from jax.sharding import PartitionSpec as P

MESH = pl.DeviceIdType.MESH

SIDE_SHARE = 0.375


def ring_order(count):
    outer = 4 if count % 4 == 0 else 1
    inner = count // outer
    if outer == 1 or inner == 1:
        return list(range(count))
    walk = [(0, 0)]
    for row in range(outer):
        columns = range(1, inner) if row % 2 == 0 else range(inner - 1, 0, -1)
        walk += [(row, column) for column in columns]
    walk += [(row, 0) for row in range(outer - 1, 0, -1)]
    return [row * inner + column for row, column in walk]


def decode_table(alive, data):
    nodes = [math.cos(math.pi * (j + 0.5) / data) for j in range(data)]
    lost = [1.0 - alive[j] for j in range(data)]
    lost_count = sum(lost)
    single = jnp.where(lost_count < 1.5, 1.0, 0.0)
    by_ones = single * alive[data]
    by_nodes = single * alive[data + 1]
    double = 1.0 - single
    table = []
    for j in range(data):
        row = [None] * (data + 2)
        gaps = [(b, double * lost[b]) for b in range(data) if b != j]
        for s in range(data):
            if s == j:
                row[s] = alive[j]
                continue
            value = -by_ones - by_nodes * (nodes[s] / nodes[j])
            for b, on in gaps:
                if b != s:
                    value = value + on * ((nodes[b] - nodes[s]) / (nodes[j] - nodes[b]))
            row[s] = lost[j] * alive[s] * value
        ones_value, nodes_value = by_ones, by_nodes * (1.0 / nodes[j])
        for b, on in gaps:
            ones_value = ones_value - on * (nodes[b] / (nodes[j] - nodes[b]))
            nodes_value = nodes_value + on * (1.0 / (nodes[j] - nodes[b]))
        row[data] = lost[j] * ones_value
        row[data + 1] = lost[j] * nodes_value
        table.append(row)
    return table


def kernel(
    codes, vocabs, order, width,
    left_ref, x_ref, w_ref, out_ref,
    lat, wbuf, enc, rx, stat_tx, stat_rx,
    w_sem, x_sem, ring_send, ring_recv, pair_send, pair_recv,
    side_send, side_recv, pass_send, pass_recv, tx_sem, rx_sem, st_send, st_recv,
):
    me = lax.axis_index("code")
    v = lax.axis_index("vocab")
    batch, depth = x_ref.shape
    share_rows = w_ref.shape[1]
    rows = batch // codes
    phases = codes // 2
    data = left_ref.shape[1]
    half = vocabs // 2
    core = lax.rem(me, 2)
    sgn = 1 - 2 * core
    partner = me + sgn
    across_y = lax.rem(me + 2, codes)

    pos = jnp.int32(0)
    for i in range(vocabs):
        pos = pos + jnp.where(v == order[i], i, 0)

    def place(shift):
        return lax.rem(pos + shift + 2 * vocabs, vocabs)

    def device_at(where):
        found = jnp.int32(0)
        for i in range(vocabs):
            found = found + jnp.where(where == i, order[i], 0)
        return found

    ahead = device_at(place(sgn))
    behind = device_at(place(-sgn))

    own_copy = pltpu.make_async_copy(x_ref, lat.at[pos], x_sem.at[0])
    own_copy.start()

    barrier = pltpu.get_barrier_semaphore()
    for k in range(1, codes):
        pl.semaphore_signal(barrier, inc=1, device_id={"code": lax.rem(me + k, codes)}, device_id_type=MESH)
    for neighbour in (ahead, behind):
        pl.semaphore_signal(barrier, inc=1, device_id={"vocab": neighbour}, device_id_type=MESH)
    pl.semaphore_wait(barrier, codes + 1)

    piece = rows // 2

    def target(phase):
        return lax.rem(me // 2 + 1 + phase, phases)

    def piece_rows(phase, sub, which):
        start = (2 * target(phase) + sub) * rows + which * piece
        return pl.ds(pl.multiple_of(start, 16), piece)

    def slot(phase, sub, way, d):
        return ((phase * 2 + sub) * 2 + way) * half + d - 1

    def ring_columns(phase):
        return pl.ds(width, depth - width) if phase == phases - 1 else pl.ds(0, depth)

    side_columns = pl.ds(0, width)

    def origin(way, d):
        return place(-sgn * d) if way == 0 else place(sgn * d)

    def move(src, dst, send, recv, device):
        return pltpu.make_async_remote_copy(
            src_ref=src, dst_ref=dst, send_sem=send, recv_sem=recv, device_id=device, device_id_type=MESH
        )

    def ring_copy(phase, sub, way, d):
        rs, cs, at = piece_rows(phase, sub, core), ring_columns(phase), slot(phase, sub, way, d)
        dst = lat.at[origin(way, d - 1), rs, cs]
        src = x_ref.at[rs, cs] if d == 1 else dst
        return move(src, dst, ring_send.at[at], ring_recv.at[at], {"vocab": ahead if way == 0 else behind})

    def arrival(phase, sub, way, d):
        at = slot(phase, sub, way, d)
        here = lat.at[origin(way, d), piece_rows(phase, sub, core), ring_columns(phase)]
        return move(here, here, ring_send.at[at], ring_recv.at[at], {"vocab": ahead if way == 0 else behind})

    def pair_copy(phase, sub, way, d):
        at = slot(phase, sub, way, d)
        here = lat.at[origin(way, d), piece_rows(phase, sub, core), ring_columns(phase)]
        return move(here, here, pair_send.at[at], pair_recv.at[at], {"code": partner})

    def pair_arrival(phase, sub, way, d):
        at = slot(phase, sub, way, d)
        here = lat.at[origin(1 - way, d), piece_rows(phase, sub, 1 - core), ring_columns(phase)]
        return move(here, here, pair_send.at[at], pair_recv.at[at], {"code": partner})

    def side_copy(sub, way, d):
        at = slot(0, sub, way, d)
        here = lat.at[origin(way, d), piece_rows(0, sub, core), side_columns]
        return move(here, here, side_send.at[at], side_recv.at[at], {"code": across_y})

    def side_arrival(sub, way, d):
        at = slot(0, sub, way, d)
        here = lat.at[origin(way, d), piece_rows(phases - 1, sub, core), side_columns]
        return move(here, here, side_send.at[at], side_recv.at[at], {"code": across_y})

    def pass_copy(sub, way, d):
        at = slot(0, sub, way, d)
        here = lat.at[origin(way, d), piece_rows(phases - 1, sub, core), side_columns]
        return move(here, here, pass_send.at[at], pass_recv.at[at], {"code": partner})

    def pass_arrival(sub, way, d):
        at = slot(0, sub, way, d)
        here = lat.at[origin(1 - way, d), piece_rows(phases - 1, sub, 1 - core), side_columns]
        return move(here, here, pass_send.at[at], pass_recv.at[at], {"code": partner})

    def reach(way):
        return half if way == 0 else half - 1

    sends = []

    def begin(phase):
        for sub in range(2):
            for way in range(2):
                if reach(way) >= 1:
                    copy = ring_copy(phase, sub, way, 1)
                    copy.start()
                    sends.append(copy)

    def multiply(phase, where, first):
        first_row = pl.multiple_of(2 * target(phase) * rows, 2 * rows)
        part = lax.dot_general(
            wbuf[where],
            lat[where, pl.ds(first_row, 2 * rows), :],
            (((1,), (1,)), ((), ())),
            preferred_element_type=jnp.float32,
        )
        for sub in range(2):
            block = 2 * target(phase) + sub
            mine = part[:, sub * rows:(sub + 1) * rows]
            enc[block] = mine if first else enc[block] + mine

    def take(phase, d):
        for sub in range(2):
            for way in range(2):
                if d <= reach(way):
                    pair_arrival(phase, sub, way, d).wait_recv()
                    if width and phase == phases - 1:
                        pass_arrival(sub, way, d).wait_recv()
        multiply(phase, place(-sgn * d), False)
        if d < half:
            multiply(phase, place(sgn * d), False)

    begin(0)
    for i in range(vocabs):
        pltpu.make_async_copy(
            w_ref.at[0, :, pl.ds(order[i] * depth, depth)], wbuf.at[i], w_sem.at[i]
        ).start()

    def pieces(d):
        return [(sub, way) for sub in range(2) for way in range(2) if d <= reach(way)]

    def receive(phase, d):
        for sub, way in pieces(d):
            arrival(phase, sub, way, d).wait_recv()
            copies = [ring_copy(phase, sub, way, d + 1)] if d < reach(way) else []
            copies.append(pair_copy(phase, sub, way, d))
            if width and phase == 0:
                copies.append(side_copy(sub, way, d))
            for copy in copies:
                copy.start()
                sends.append(copy)
        if d == max(half - 1, 1) and phase + 1 < phases:
            begin(phase + 1)

    def hand_on(phase, d):
        if width and phase == 0:
            for sub, way in pieces(d):
                side_arrival(sub, way, d).wait_recv()
                copy = pass_copy(sub, way, d)
                copy.start()
                sends.append(copy)

    def deliver(phase):
        there = 2 * target(phase)
        for block in (there, there + 1) if phase < phases - 1 else (partner,):
            move(enc.at[block], rx.at[me], tx_sem.at[block], rx_sem.at[me], {"code": block}).start()

    steps = [(phase, d) for phase in range(phases) for d in range(1, half + 1)]
    for t in range(len(steps) + 2):
        if t < len(steps):
            receive(*steps[t])
        if 1 <= t <= len(steps):
            hand_on(*steps[t - 1])
        if t == 2:
            own_copy.wait()
            for i in range(vocabs):
                pltpu.make_async_copy(
                    w_ref.at[0, :, pl.ds(order[i] * depth, depth)], wbuf.at[i], w_sem.at[i]
                ).wait()
        if t >= 2:
            phase, d = steps[t - 2]
            if d == 1:
                multiply(phase, pos, True)
            take(phase, d)
            if d == half:
                deliver(phase)

    rx[me] = enc[me]

    alive = []
    for s in range(codes):
        here = jnp.int32(0)
        for k in range(data):
            here = here + jnp.where(left_ref[0, k] == s, 1, 0)
        alive.append(here.astype(jnp.float32))
    table = decode_table(alive, data)

    for k in range(1, codes):
        other = lax.rem(me + k, codes)
        pltpu.make_async_remote_copy(
            src_ref=enc.at[0],
            dst_ref=rx.at[other],
            send_sem=tx_sem.at[other],
            recv_sem=rx_sem.at[other],
            device_id={"code": other},
            device_id_type=MESH,
        ).wait_recv()

    top = None
    logits = []
    for j in range(data):
        value = table[j][0] * rx[0]
        for s in range(1, codes):
            value = value + table[j][s] * rx[s]
        logits.append(value)
        out_ref[j * share_rows:(j + 1) * share_rows, :] = value
        peak = jnp.max(value, axis=0, keepdims=True)
        top = peak if top is None else jnp.maximum(top, peak)
    total = None
    for j in range(data):
        part = jnp.sum(jnp.exp(logits[j] - top), axis=0, keepdims=True)
        total = part if total is None else total + part

    line = lax.broadcasted_iota(jnp.int32, (8, rows), 0)
    stat_tx[...] = jnp.where(line == 0, top, total)
    stat_rx[v] = stat_tx[...]
    stat_sends = []
    for k in range(1, vocabs):
        copy = pltpu.make_async_remote_copy(
            src_ref=stat_tx,
            dst_ref=stat_rx.at[v],
            send_sem=st_send.at[k],
            recv_sem=st_recv.at[v],
            device_id={"vocab": lax.rem(v + k, vocabs)},
            device_id_type=MESH,
        )
        copy.start()
        stat_sends.append(copy)
    for copy in sends:
        copy.wait_send()
    for k in range(1, codes):
        other = lax.rem(me + k, codes)
        pltpu.make_async_remote_copy(
            src_ref=enc.at[0],
            dst_ref=rx.at[other],
            send_sem=tx_sem.at[other],
            recv_sem=rx_sem.at[other],
            device_id={"code": other},
            device_id_type=MESH,
        ).wait_send()
    for k in range(1, vocabs):
        other = lax.rem(v + k, vocabs)
        pltpu.make_async_remote_copy(
            src_ref=stat_tx,
            dst_ref=stat_rx.at[other],
            send_sem=st_send.at[k],
            recv_sem=st_recv.at[other],
            device_id={"vocab": other},
            device_id_type=MESH,
        ).wait_recv()

    stats = stat_rx[...]
    tops, totals = stats[:, 0:1, :], stats[:, 1:2, :]
    peak = jnp.max(tops, axis=0)
    whole = jnp.sum(totals * jnp.exp(tops - peak[None]), axis=0)
    out_ref[...] = out_ref[...] - (peak + jnp.log(whole))
    for copy in stat_sends:
        copy.wait_send()


def solution(mesh):
    codes, vocabs = mesh.shape["code"], mesh.shape["vocab"]
    order = ring_order(vocabs)

    def shards(latent_activations, code_fragments, remaining_fragments):
        batch, depth = latent_activations.shape
        share_rows = code_fragments.shape[1]
        data = remaining_fragments.shape[1]
        rows = batch // codes
        width = int(depth * SIDE_SHARE) // 128 * 128 if codes == 4 else 0
        slots = (codes // 2) * 2 * 2 * (vocabs // 2)
        dma = pltpu.SemaphoreType.DMA
        return pl.pallas_call(
            functools.partial(kernel, codes, vocabs, order, width),
            out_shape=jax.ShapeDtypeStruct((data * share_rows, rows), jnp.float32),
            in_specs=[
                pl.BlockSpec(memory_space=pltpu.SMEM),
                pl.BlockSpec(memory_space=pl.ANY),
                pl.BlockSpec(memory_space=pl.ANY),
            ],
            out_specs=pl.BlockSpec(memory_space=pltpu.VMEM),
            scratch_shapes=[
                pltpu.VMEM((vocabs, batch, depth), jnp.bfloat16),
                pltpu.VMEM((vocabs, share_rows, depth), jnp.bfloat16),
                pltpu.VMEM((codes, share_rows, rows), jnp.float32),
                pltpu.VMEM((codes, share_rows, rows), jnp.float32),
                pltpu.VMEM((8, rows), jnp.float32),
                pltpu.VMEM((vocabs, 8, rows), jnp.float32),
                dma((vocabs,)),
                dma((1,)),
                *[dma((slots,)) for _ in range(8)],
                dma((codes,)),
                dma((codes,)),
                dma((vocabs,)),
                dma((vocabs,)),
            ],
            compiler_params=pltpu.CompilerParams(collective_id=0, has_side_effects=True),
        )(remaining_fragments, latent_activations, code_fragments).T

    return jax.shard_map(
        shards,
        mesh=mesh,
        in_specs=(P(None, "vocab"), P("code", "vocab", None), P("vocab", None)),
        out_specs=P("code", "vocab"),
        check_vma=False,
    )
```

```python
import functools
import math

import jax
import jax.numpy as jnp
from jax import lax
from jax.experimental import pallas as pl
from jax.experimental.pallas import tpu as pltpu
from jax.sharding import PartitionSpec as P

MESH = pl.DeviceIdType.MESH

SIDE_SHARE = 0.5


def ring_order(count):
    outer = 4 if count % 4 == 0 else 1
    inner = count // outer
    if outer == 1 or inner == 1:
        return list(range(count))
    walk = [(0, 0)]
    for row in range(outer):
        columns = range(1, inner) if row % 2 == 0 else range(inner - 1, 0, -1)
        walk += [(row, column) for column in columns]
    walk += [(row, 0) for row in range(outer - 1, 0, -1)]
    return [row * inner + column for row, column in walk]


def decode_table(alive, data):
    nodes = [math.cos(math.pi * (j + 0.5) / data) for j in range(data)]
    lost = [1.0 - alive[j] for j in range(data)]
    lost_count = sum(lost)
    single = jnp.where(lost_count < 1.5, 1.0, 0.0)
    by_ones = single * alive[data]
    by_nodes = single * alive[data + 1]
    double = 1.0 - single
    table = []
    for j in range(data):
        row = [None] * (data + 2)
        gaps = [(b, double * lost[b]) for b in range(data) if b != j]
        for s in range(data):
            if s == j:
                row[s] = alive[j]
                continue
            value = -by_ones - by_nodes * (nodes[s] / nodes[j])
            for b, on in gaps:
                if b != s:
                    value = value + on * ((nodes[b] - nodes[s]) / (nodes[j] - nodes[b]))
            row[s] = lost[j] * alive[s] * value
        ones_value, nodes_value = by_ones, by_nodes * (1.0 / nodes[j])
        for b, on in gaps:
            ones_value = ones_value - on * (nodes[b] / (nodes[j] - nodes[b]))
            nodes_value = nodes_value + on * (1.0 / (nodes[j] - nodes[b]))
        row[data] = lost[j] * ones_value
        row[data + 1] = lost[j] * nodes_value
        table.append(row)
    return table


def kernel(
    codes, vocabs, order, width,
    left_ref, x_ref, w_ref, out_ref,
    lat, wbuf, enc, rx, stat_tx, stat_rx,
    w_sem, x_sem, ring_send, ring_recv, pair_send, pair_recv,
    side_send, side_recv, pass_send, pass_recv, tx_sem, rx_sem, st_send, st_recv,
):
    me = lax.axis_index("code")
    v = lax.axis_index("vocab")
    batch, depth = x_ref.shape
    share_rows = w_ref.shape[1]
    rows = batch // codes
    phases = codes // 2
    data = left_ref.shape[1]
    half = vocabs // 2
    core = lax.rem(me, 2)
    sgn = 1 - 2 * core
    partner = me + sgn
    across_y = lax.rem(me + 2, codes)

    pos = jnp.int32(0)
    for i in range(vocabs):
        pos = pos + jnp.where(v == order[i], i, 0)

    def place(shift):
        return lax.rem(pos + shift + 2 * vocabs, vocabs)

    def device_at(where):
        found = jnp.int32(0)
        for i in range(vocabs):
            found = found + jnp.where(where == i, order[i], 0)
        return found

    ahead = device_at(place(sgn))
    behind = device_at(place(-sgn))

    own_copy = pltpu.make_async_copy(x_ref, lat.at[pos], x_sem.at[0])
    own_copy.start()

    barrier = pltpu.get_barrier_semaphore()
    for k in range(1, codes):
        pl.semaphore_signal(barrier, inc=1, device_id={"code": lax.rem(me + k, codes)}, device_id_type=MESH)
    for neighbour in (ahead, behind):
        pl.semaphore_signal(barrier, inc=1, device_id={"vocab": neighbour}, device_id_type=MESH)
    pl.semaphore_wait(barrier, codes + 1)

    piece = rows // 2

    def target(phase):
        return lax.rem(me // 2 + 1 + phase, phases)

    def piece_rows(phase, sub, which):
        start = (2 * target(phase) + sub) * rows + which * piece
        return pl.ds(pl.multiple_of(start, 16), piece)

    def slot(phase, sub, way, d):
        return ((phase * 2 + sub) * 2 + way) * half + d - 1

    def ring_columns(phase):
        return pl.ds(width, depth - width) if phase == phases - 1 else pl.ds(0, depth)

    side_columns = pl.ds(0, width)

    def origin(way, d):
        return place(-sgn * d) if way == 0 else place(sgn * d)

    def move(src, dst, send, recv, device):
        return pltpu.make_async_remote_copy(
            src_ref=src, dst_ref=dst, send_sem=send, recv_sem=recv, device_id=device, device_id_type=MESH
        )

    def ring_copy(phase, sub, way, d):
        rs, cs, at = piece_rows(phase, sub, core), ring_columns(phase), slot(phase, sub, way, d)
        dst = lat.at[origin(way, d - 1), rs, cs]
        src = x_ref.at[rs, cs] if d == 1 else dst
        return move(src, dst, ring_send.at[at], ring_recv.at[at], {"vocab": ahead if way == 0 else behind})

    def arrival(phase, sub, way, d):
        at = slot(phase, sub, way, d)
        here = lat.at[origin(way, d), piece_rows(phase, sub, core), ring_columns(phase)]
        return move(here, here, ring_send.at[at], ring_recv.at[at], {"vocab": ahead if way == 0 else behind})

    def pair_copy(phase, sub, way, d):
        at = slot(phase, sub, way, d)
        here = lat.at[origin(way, d), piece_rows(phase, sub, core), ring_columns(phase)]
        return move(here, here, pair_send.at[at], pair_recv.at[at], {"code": partner})

    def pair_arrival(phase, sub, way, d):
        at = slot(phase, sub, way, d)
        here = lat.at[origin(1 - way, d), piece_rows(phase, sub, 1 - core), ring_columns(phase)]
        return move(here, here, pair_send.at[at], pair_recv.at[at], {"code": partner})

    def side_copy(sub, way, d):
        at = slot(0, sub, way, d)
        here = lat.at[origin(way, d), piece_rows(0, sub, core), side_columns]
        return move(here, here, side_send.at[at], side_recv.at[at], {"code": across_y})

    def side_arrival(sub, way, d):
        at = slot(0, sub, way, d)
        here = lat.at[origin(way, d), piece_rows(phases - 1, sub, core), side_columns]
        return move(here, here, side_send.at[at], side_recv.at[at], {"code": across_y})

    def pass_copy(sub, way, d):
        at = slot(0, sub, way, d)
        here = lat.at[origin(way, d), piece_rows(phases - 1, sub, core), side_columns]
        return move(here, here, pass_send.at[at], pass_recv.at[at], {"code": partner})

    def pass_arrival(sub, way, d):
        at = slot(0, sub, way, d)
        here = lat.at[origin(1 - way, d), piece_rows(phases - 1, sub, 1 - core), side_columns]
        return move(here, here, pass_send.at[at], pass_recv.at[at], {"code": partner})

    def reach(way):
        return half if way == 0 else half - 1

    sends = []

    def begin(phase):
        for sub in range(2):
            for way in range(2):
                if reach(way) >= 1:
                    copy = ring_copy(phase, sub, way, 1)
                    copy.start()
                    sends.append(copy)

    def multiply(phase, where, first):
        first_row = pl.multiple_of(2 * target(phase) * rows, 2 * rows)
        part = lax.dot_general(
            wbuf[where],
            lat[where, pl.ds(first_row, 2 * rows), :],
            (((1,), (1,)), ((), ())),
            preferred_element_type=jnp.float32,
        )
        for sub in range(2):
            block = 2 * target(phase) + sub
            mine = part[:, sub * rows:(sub + 1) * rows]
            enc[block] = mine if first else enc[block] + mine

    def take(phase, d):
        for sub in range(2):
            for way in range(2):
                if d <= reach(way):
                    pair_arrival(phase, sub, way, d).wait_recv()
                    if width and phase == phases - 1:
                        pass_arrival(sub, way, d).wait_recv()
        multiply(phase, place(-sgn * d), False)
        if d < half:
            multiply(phase, place(sgn * d), False)

    begin(0)
    for i in range(vocabs):
        pltpu.make_async_copy(
            w_ref.at[0, :, pl.ds(order[i] * depth, depth)], wbuf.at[i], w_sem.at[i]
        ).start()

    def pieces(d):
        return [(sub, way) for sub in range(2) for way in range(2) if d <= reach(way)]

    def receive(phase, d):
        for sub, way in pieces(d):
            arrival(phase, sub, way, d).wait_recv()
            copies = [ring_copy(phase, sub, way, d + 1)] if d < reach(way) else []
            copies.append(pair_copy(phase, sub, way, d))
            if width and phase == 0:
                copies.append(side_copy(sub, way, d))
            for copy in copies:
                copy.start()
                sends.append(copy)
        if d == max(half - 1, 1) and phase + 1 < phases:
            begin(phase + 1)

    def hand_on(phase, d):
        if width and phase == 0:
            for sub, way in pieces(d):
                side_arrival(sub, way, d).wait_recv()
                copy = pass_copy(sub, way, d)
                copy.start()
                sends.append(copy)

    def deliver(phase):
        there = 2 * target(phase)
        for block in (there, there + 1) if phase < phases - 1 else (partner,):
            move(enc.at[block], rx.at[me], tx_sem.at[block], rx_sem.at[me], {"code": block}).start()

    steps = [(phase, d) for phase in range(phases) for d in range(1, half + 1)]
    for t, (phase, d) in enumerate(steps):
        receive(phase, d)
        if t == min(1, half - 1):
            own_copy.wait()
            for i in range(vocabs):
                pltpu.make_async_copy(
                    w_ref.at[0, :, pl.ds(order[i] * depth, depth)], wbuf.at[i], w_sem.at[i]
                ).wait()
        if d > 1:
            if d == 2:
                multiply(phase, pos, True)
            take(phase, d - 1)
        if d == half:
            if d == 1:
                multiply(phase, pos, True)
            take(phase, d)
            deliver(phase)
        if d > 1:
            hand_on(phase, d - 1)
        if d == half:
            hand_on(phase, d)

    rx[me] = enc[me]

    alive = []
    for s in range(codes):
        here = jnp.int32(0)
        for k in range(data):
            here = here + jnp.where(left_ref[0, k] == s, 1, 0)
        alive.append(here.astype(jnp.float32))
    table = decode_table(alive, data)

    for k in range(1, codes):
        other = lax.rem(me + k, codes)
        pltpu.make_async_remote_copy(
            src_ref=enc.at[0],
            dst_ref=rx.at[other],
            send_sem=tx_sem.at[other],
            recv_sem=rx_sem.at[other],
            device_id={"code": other},
            device_id_type=MESH,
        ).wait_recv()

    top = None
    logits = []
    for j in range(data):
        value = table[j][0] * rx[0]
        for s in range(1, codes):
            value = value + table[j][s] * rx[s]
        logits.append(value)
        out_ref[j * share_rows:(j + 1) * share_rows, :] = value
        peak = jnp.max(value, axis=0, keepdims=True)
        top = peak if top is None else jnp.maximum(top, peak)
    total = None
    for j in range(data):
        part = jnp.sum(jnp.exp(logits[j] - top), axis=0, keepdims=True)
        total = part if total is None else total + part

    line = lax.broadcasted_iota(jnp.int32, (8, rows), 0)
    stat_tx[...] = jnp.where(line == 0, top, total)
    stat_rx[v] = stat_tx[...]
    stat_sends = []
    for k in range(1, vocabs):
        copy = pltpu.make_async_remote_copy(
            src_ref=stat_tx,
            dst_ref=stat_rx.at[v],
            send_sem=st_send.at[k],
            recv_sem=st_recv.at[v],
            device_id={"vocab": lax.rem(v + k, vocabs)},
            device_id_type=MESH,
        )
        copy.start()
        stat_sends.append(copy)
    for copy in sends:
        copy.wait_send()
    for k in range(1, codes):
        other = lax.rem(me + k, codes)
        pltpu.make_async_remote_copy(
            src_ref=enc.at[0],
            dst_ref=rx.at[other],
            send_sem=tx_sem.at[other],
            recv_sem=rx_sem.at[other],
            device_id={"code": other},
            device_id_type=MESH,
        ).wait_send()
    for k in range(1, vocabs):
        other = lax.rem(v + k, vocabs)
        pltpu.make_async_remote_copy(
            src_ref=stat_tx,
            dst_ref=stat_rx.at[other],
            send_sem=st_send.at[k],
            recv_sem=st_recv.at[other],
            device_id={"vocab": other},
            device_id_type=MESH,
        ).wait_recv()

    stats = stat_rx[...]
    tops, totals = stats[:, 0:1, :], stats[:, 1:2, :]
    peak = jnp.max(tops, axis=0)
    whole = jnp.sum(totals * jnp.exp(tops - peak[None]), axis=0)
    out_ref[...] = out_ref[...] - (peak + jnp.log(whole))
    for copy in stat_sends:
        copy.wait_send()


def solution(mesh):
    codes, vocabs = mesh.shape["code"], mesh.shape["vocab"]
    order = ring_order(vocabs)

    def shards(latent_activations, code_fragments, remaining_fragments):
        batch, depth = latent_activations.shape
        share_rows = code_fragments.shape[1]
        data = remaining_fragments.shape[1]
        rows = batch // codes
        width = int(depth * SIDE_SHARE) // 128 * 128 if codes == 4 else 0
        slots = (codes // 2) * 2 * 2 * (vocabs // 2)
        dma = pltpu.SemaphoreType.DMA
        return pl.pallas_call(
            functools.partial(kernel, codes, vocabs, order, width),
            out_shape=jax.ShapeDtypeStruct((data * share_rows, rows), jnp.float32),
            in_specs=[
                pl.BlockSpec(memory_space=pltpu.SMEM),
                pl.BlockSpec(memory_space=pl.ANY),
                pl.BlockSpec(memory_space=pl.ANY),
            ],
            out_specs=pl.BlockSpec(memory_space=pltpu.VMEM),
            scratch_shapes=[
                pltpu.VMEM((vocabs, batch, depth), jnp.bfloat16),
                pltpu.VMEM((vocabs, share_rows, depth), jnp.bfloat16),
                pltpu.VMEM((codes, share_rows, rows), jnp.float32),
                pltpu.VMEM((codes, share_rows, rows), jnp.float32),
                pltpu.VMEM((8, rows), jnp.float32),
                pltpu.VMEM((vocabs, 8, rows), jnp.float32),
                dma((vocabs,)),
                dma((1,)),
                *[dma((slots,)) for _ in range(8)],
                dma((codes,)),
                dma((codes,)),
                dma((vocabs,)),
                dma((vocabs,)),
            ],
            compiler_params=pltpu.CompilerParams(collective_id=0, has_side_effects=True),
        )(remaining_fragments, latent_activations, code_fragments).T

    return jax.shard_map(
        shards,
        mesh=mesh,
        in_specs=(P(None, "vocab"), P("code", "vocab", None), P("vocab", None)),
        out_specs=P("code", "vocab"),
        check_vma=False,
    )
```
